256 devices in a mesh: pipe: 2 (over x_hi), dp: 128 (over x_lo, z, y, core).
Axes of the slice: x: 4 (x_hi: 2, x_lo: 2; x = x_hi * 2 + x_lo), y: 4, z: 8, core: 2. Of those that a mesh axis runs over, the one named last changes fastest.
Arguments:
- images: bfloat16 [256, 1024, 384], P('dp'), may hold values from -6 to 6
- dw_kernel: bfloat16 [2, 49, 384], P('pipe'), may hold values from -0.875 to 0.875
- dw_bias: bfloat16 [2, 384], P('pipe'), may hold values from -3 to 3
- norm_gain: bfloat16 [2, 384], P('pipe'), may hold values from 0.5 to 1.5
- norm_bias: bfloat16 [2, 384], P('pipe'), may hold values from -3 to 3
- w_in: bfloat16 [2, 384, 1536], P('pipe'), may hold values from -0.3125 to 0.3125
- b_in: bfloat16 [2, 1536], P('pipe'), may hold values from -3 to 3
- w_out: bfloat16 [2, 1536, 384], P('pipe'), may hold values from -0.15625 to 0.15625
- b_out: bfloat16 [2, 384], P('pipe'), may hold values from -3 to 3
- layer_scale: bfloat16 [2, 384], P('pipe'), may hold values from 0.29882812 to 1
- image_embed: bfloat16 [1024, 1024], P(('pipe', 'dp')), may hold values from -8 to 8
- text_embed: bfloat16 [1024, 1024], P('dp'), may hold values from -8 to 8
Outputs:
- section_out: bfloat16 [2, 256, 1024, 384], P('pipe', 'dp')
- row_lse: float32 [1024], P(('pipe', 'dp'))
- col_lse: float32 [1024], P('dp')
- grad_image: float32 [1024, 1024], P(('pipe', 'dp'))
- grad_text: float32 [1024, 1024], P('dp')
The draws below stay inside these ranges and needn't reach their ends.
All inputs are finite; a program needn't handle non-finite values.
Results may differ from the reference program's by a relative error of at most 0.0055.
Values may be sent and summed in bfloat16 or wider, within the bound.
A program may use at most 128 MiB of HBM per device.

```python
import jax
import jax.numpy as jnp
from jax import lax

C = 384
HID = 1536
E = 1024
KS = 7
SIDE = 32
MICRO = 2
PAIRS = 1024
N_PIPE = 2
N_DP = 128


def text_base(key):
    sub = jax.random.fold_in(key, 7)
    return jnp.clip(jax.random.normal(sub, (PAIRS, E), jnp.float32), -6.0, 6.0)


def draw_text_embed(key, part):
    return text_base(key).astype(jnp.bfloat16)


def draw_image_embed(key, part):
    own = jnp.clip(jax.random.normal(jax.random.fold_in(key, 11), (PAIRS, E), jnp.float32), -4.0, 4.0)
    return own.astype(jnp.bfloat16)


def block_scale(key, extent, shards, smallest, high):
    def one(position, blocks):
        heights = jax.random.uniform(jax.random.fold_in(jax.random.fold_in(key, 6), position), (blocks,), jnp.float32, smallest / len(shards), high / len(shards))
        return jnp.repeat(jnp.exp(heights), extent[position] // blocks).reshape((-1,) + (1,) * (len(extent) - position - 1))

    level = one(*shards[0])
    for cut in shards[1:]:
        level = level * one(*cut)
    return level


def centred(stream_key, dims, scale, limit, pieces=(), kind=jnp.bfloat16):
    array = jax.random.normal(stream_key, dims, jnp.float32) * scale
    if len(pieces) > 0:
        array = block_scale(stream_key, dims, pieces, -0.22, 0.18) * array
    return jnp.clip(array, min=-limit, max=limit).astype(kind)


def setup_inputs(seed: int = 0) -> dict:
    keys = jax.random.split(jax.random.key(seed), 13)
    return {
        "images": centred(keys[0], (N_DP * MICRO, SIDE * SIDE, C), 1.0, 6.0, ((0, 128),)),
        "dw_kernel": centred(keys[1], (N_PIPE, KS * KS, C), (KS * KS) ** -0.5, 0.875, ((0, 2),)),
        "dw_bias": centred(keys[2], (N_PIPE, C), 0.5, 3.0, ((0, 2),)),
        "norm_gain": jnp.clip(1.0 + 0.1 * jax.random.normal(keys[3], (N_PIPE, C), jnp.float32), 0.5, 1.5).astype(jnp.bfloat16),
        "norm_bias": centred(keys[4], (N_PIPE, C), 0.5, 3.0, ((0, 2),)),
        "w_in": centred(keys[5], (N_PIPE, C, HID), C ** -0.5, 0.3125, ((0, 2),)),
        "b_in": centred(keys[6], (N_PIPE, HID), 0.5, 3.0, ((0, 2),)),
        "w_out": centred(keys[7], (N_PIPE, HID, C), HID ** -0.5, 0.15625, ((0, 2),)),
        "b_out": centred(keys[8], (N_PIPE, C), 0.5, 3.0, ((0, 2),)),
        "layer_scale": jnp.clip(0.29882812 + 0.7011719 * jax.random.uniform(keys[9], (N_PIPE, C), jnp.float32) ** block_scale(keys[9], (N_PIPE, C), ((0, 2),), -0.2, 0.2), 0.29882812, 1.0).astype(jnp.bfloat16),
        "image_embed": draw_image_embed(jax.random.fold_in(keys[12], 71), 0),
        "text_embed": draw_text_embed(jax.random.fold_in(keys[12], 71), 0),
    }


def convnext_block(feature, params, side):
    dw_kernel, dw_bias, norm_gain, norm_bias, w_in, b_in, w_out, b_out, layer_scale = params
    count, positions, channels = feature.shape
    taps = dw_kernel.shape[0]
    width = 1
    while width * width < taps:
        width = width + 1
    grid = feature.reshape(count, side, side, channels)
    kernel = dw_kernel.reshape(width, width, 1, channels)
    conv = lax.conv_general_dilated(grid, kernel, (1, 1), ((width // 2, width // 2), (width // 2, width // 2)), dimension_numbers=('NHWC', 'HWIO', 'NHWC'), feature_group_count=channels, preferred_element_type=jnp.float32)
    conv = conv.reshape(count * positions, channels) + dw_bias.astype(jnp.float32)
    center = conv - lax.optimization_barrier(jnp.mean(conv, axis=1, keepdims=True))
    spread = lax.optimization_barrier(jnp.mean(center * center, axis=1, keepdims=True))
    normed = (center * lax.rsqrt(spread + 1e-06) * norm_gain.astype(jnp.float32) + norm_bias.astype(jnp.float32)).astype(jnp.bfloat16)
    hidden = jnp.dot(normed, w_in, preferred_element_type=jnp.float32) + b_in.astype(jnp.float32)
    hidden = jax.nn.gelu(hidden, approximate=False).astype(jnp.bfloat16)
    branch = jnp.dot(hidden, w_out, preferred_element_type=jnp.float32) + b_out.astype(jnp.float32)
    result = feature.reshape(count * positions, channels).astype(jnp.float32) + layer_scale.astype(jnp.float32) * branch
    return result.astype(jnp.bfloat16).reshape(count, positions, channels)

def unit_rows(values):
    wide = values.astype(jnp.float32)
    return (wide * lax.rsqrt(lax.optimization_barrier(jnp.sum(wide * wide, axis=1, keepdims=True)) + 1e-06)).astype(jnp.bfloat16)

def reference(images, dw_kernel, dw_bias, norm_gain, norm_bias, w_in, b_in, w_out, b_out, layer_scale, image_embed, text_embed):
    every = (dw_kernel, dw_bias, norm_gain, norm_bias, w_in, b_in, w_out, b_out, layer_scale)
    outputs = []
    current = images
    for section in range(N_PIPE):
        params = tuple((p[section] for p in every))
        current = lax.map(lambda one: convnext_block(one[None], params, SIDE)[0], current)
        outputs.append(current)
    section_out = jnp.stack(outputs)
    image_unit = unit_rows(image_embed)
    text_unit = unit_rows(text_embed)
    logits = 100.0 * jnp.dot(image_unit, text_unit.T, preferred_element_type=jnp.float32)
    row_top = lax.optimization_barrier(jnp.max(logits, axis=1))
    row_lse = row_top + jnp.log(lax.optimization_barrier(jnp.sum(jnp.exp(logits - row_top[:, None]), axis=1)))
    col_top = lax.optimization_barrier(jnp.max(logits, axis=0))
    col_lse = col_top + jnp.log(lax.optimization_barrier(jnp.sum(jnp.exp(logits - col_top[None, :]), axis=0)))
    eye = jnp.eye(PAIRS, dtype=jnp.float32)
    dlogits = (jnp.exp(logits - row_lse[:, None]) + jnp.exp(logits - col_lse[None, :]) - 2.0 * eye).astype(jnp.bfloat16)
    grad_image = 100.0 * jnp.dot(dlogits, text_unit, preferred_element_type=jnp.float32)
    grad_text = 100.0 * jnp.dot(dlogits.T, image_unit, preferred_element_type=jnp.float32)
    return (section_out, row_lse, col_lse, grad_image, grad_text)
```

```python
import functools

import jax
import jax.numpy as jnp
from jax import lax
from jax.experimental import pallas as pl
from jax.experimental.pallas import tpu as pltpu
from jax.sharding import PartitionSpec as P

MESH = pl.DeviceIdType.MESH
F32 = jnp.float32
BF16 = jnp.bfloat16

N_Z, N_Y = 8, 4
GROUP = 16
SIDE = 32
LANES = 128
STRIP = 8
STRIPS = SIDE // STRIP
POS = STRIP * SIDE
LEFT = 8
CHUNK = 256


def kernel(
    images, dw_kernel, dw_bias, norm_gain, norm_bias, w_in, b_in, w_out, b_out, layer_scale,
    image_embed, text_embed,
    out, row_out, col_out, grad_image, grad_text,
    src, outbuf, xpad, taps, conv, normed, branch, w_in_v, w_out_v,
    imgbuf, txtbuf, imgf, img2, txt2, logit, logit_t, rowst, colst,
    gi_send, gi_recv, gt_send, gt_recv, gt_half, gt_other,
    load_sem, store_sem, strip_send, strip_recv, img_send, img_recv, txt_send, txt_recv,
    row_send, row_recv, col_send, col_recv, gis_sem, gir_sem, gts_sem, gtr_sem, half_send, half_recv,
):
    sec = lax.axis_index("pipe")
    dp = lax.axis_index("dp")
    core = lax.rem(dp, 2)
    y = lax.rem(lax.div(dp, 2), N_Y)
    z = lax.rem(lax.div(dp, 2 * N_Y), N_Z)
    x_lo = lax.div(dp, 2 * N_Y * N_Z)
    me_row = x_lo * 8 + y * 2 + core
    me_col = sec * N_Z + z
    micro = src.shape[0]
    channels = src.shape[2]
    tiles = channels // LANES
    hidden = w_in_v.shape[1]
    total = micro * STRIPS

    def row_peer(j):
        return (sec, ((lax.div(j, 8) * N_Z + z) * N_Y + lax.rem(lax.div(j, 2), N_Y)) * 2 + lax.rem(j, 2))

    def col_peer(j):
        return (lax.div(j, N_Z), ((x_lo * N_Z + lax.rem(j, N_Z)) * N_Y + y) * 2 + core)

    def text_peer(j):
        return (sec, ((x_lo * N_Z + j) * N_Y + y) * 2 + core)

    partner = (1 - sec, dp)

    def remote(source, target, send, recv, device):
        return pltpu.make_async_remote_copy(
            src_ref=source, dst_ref=target, send_sem=send, recv_sem=recv,
            device_id=device, device_id_type=MESH,
        )

    def others(count, me, act):
        def one(j, carry):
            @pl.when(j != me)
            def _():
                act(j)
            return carry
        lax.fori_loop(0, count, one, 0)

    load_x = pltpu.make_async_copy(images, src, load_sem.at[0])
    load_a = pltpu.make_async_copy(w_in.at[0], w_in_v, load_sem.at[1])
    load_b = pltpu.make_async_copy(w_out.at[0], w_out_v, load_sem.at[2])

    @pl.when(sec == 0)
    def _():
        load_x.start()
    load_a.start()
    load_b.start()

    barrier = pltpu.get_barrier_semaphore()
    others(GROUP, me_row, lambda j: pl.semaphore_signal(
        barrier, inc=1, device_id=row_peer(j), device_id_type=MESH))
    others(GROUP, me_col, lambda j: pl.semaphore_signal(
        barrier, inc=1, device_id=col_peer(j), device_id_type=MESH))

    def unit(values):
        wide = values.astype(F32)
        return (wide * lax.rsqrt(jnp.sum(wide * wide, axis=1, keepdims=True) + 1e-06)).astype(BF16)

    imgbuf[me_row] = unit(image_embed[...])
    txtbuf[z] = unit(text_embed[...])

    xpad[:, :, 0:3] = jnp.zeros(xpad.shape[:2] + (3,) + xpad.shape[3:], F32)
    xpad[:, :, SIDE + 3:SIDE + 6] = jnp.zeros(xpad.shape[:2] + (3,) + xpad.shape[3:], F32)
    xpad[:, :, :, 0:LEFT] = jnp.zeros(xpad.shape[:3] + (LEFT, LANES), F32)
    xpad[:, :, :, LEFT + SIDE:] = jnp.zeros(xpad.shape[:3] + (8, LANES), F32)
    kv = dw_kernel[0].astype(F32)
    for c in range(tiles):
        for t in range(49):
            taps[c, t] = jnp.broadcast_to(kv[t:t + 1, c * LANES:(c + 1) * LANES], (8, LANES))

    pl.semaphore_wait(barrier, 2 * (GROUP - 1))

    def img_copy(slot, j):
        return remote(imgbuf.at[slot], imgbuf.at[slot], img_send.at[j], img_recv.at[slot], row_peer(j))

    def txt_copy(slot, j):
        return remote(txtbuf.at[slot], txtbuf.at[slot], txt_send.at[j], txt_recv.at[slot], text_peer(j))

    def row_copy(slot, j):
        return remote(rowst.at[slot], rowst.at[slot], row_send.at[j], row_recv.at[slot], row_peer(j))

    def col_copy(slot, j):
        return remote(colst.at[slot], colst.at[slot], col_send.at[j], col_recv.at[slot], col_peer(j))

    def gi_copy(slot, j):
        return remote(gi_send.at[j], gi_recv.at[slot], gis_sem.at[j], gir_sem.at[slot], row_peer(j))

    def gt_copy(slot, j):
        return remote(gt_send.at[j], gt_recv.at[slot], gts_sem.at[j], gtr_sem.at[slot], text_peer(j))

    half_copy = remote(gt_half, gt_other, half_send, half_recv, partner)

    others(GROUP, me_row, lambda j: img_copy(me_row, j).start())
    others(N_Z, z, lambda j: txt_copy(z, j).start())

    def finish(copy):
        copy.wait_send()
        copy.wait_recv()

    lane = lax.broadcasted_iota(jnp.int32, (1, LANES), 1)
    low = lane < 64

    def loss_logits():
        others(GROUP, me_row, lambda j: finish(img_copy(j, j)))
        others(N_Z, z, lambda j: finish(txt_copy(j, j)))
        for j in range(GROUP):
            imgf[4 * j:4 * j + 4] = imgbuf[j].astype(F32)
        img = imgf[...].astype(BF16)
        img2[0:64] = img
        img2[64:128] = img
        for j in range(N_Z):
            imgf[8 * j:8 * j + 8] = txtbuf[j].astype(F32)
        txt = imgf[...].astype(BF16)
        txt2[0:64] = txt
        txt2[64:128] = txt
        dims = (((1,), (1,)), ((), ()))
        a = 100.0 * lax.dot_general(img2[0:64], txt2[...], dims, preferred_element_type=F32)
        b = 100.0 * lax.dot_general(txt2[0:64], img2[...], dims, preferred_element_type=F32)
        logit[...] = a
        logit_t[...] = b

        def stats(values):
            top = jnp.max(values, axis=0, keepdims=True)
            return jnp.where(low, top, jnp.sum(jnp.exp(values - top), axis=0, keepdims=True))

        colst[me_col] = stats(a)
        rowst[me_row] = stats(b)
        others(GROUP, me_row, lambda j: row_copy(me_row, j).start())
        others(GROUP, me_col, lambda j: col_copy(me_col, j).start())

    def merged(ref):
        parts = [ref[j] for j in range(GROUP)]
        top = functools.reduce(jnp.maximum, parts)
        add = functools.reduce(
            jnp.add, [pltpu.roll(p, 64, 1) * jnp.exp(jnp.where(low, p - top, 0.0)) for p in parts])
        lse = top + jnp.log(jnp.where(low, add, 1.0))
        return jnp.where(low, lse, pltpu.roll(lse, 64, 1))

    def upright(row):
        here = lax.broadcasted_iota(jnp.int32, (64, LANES), 0) == lax.broadcasted_iota(jnp.int32, (64, LANES), 1)
        return jnp.sum(jnp.where(here, row, 0.0), axis=1, keepdims=True)

    def image_ids(r):
        j = r >> 2
        peer = (((j >> 3) * N_Z + z) * N_Y + ((j >> 1) & 3)) * 2 + (j & 1)
        return (sec * 128 + peer) * 4 + (r & 3)

    def text_ids(r):
        return (((x_lo * N_Z + (r >> 3)) * N_Y + y) * 2 + core) * 8 + (r & 7)

    def loss_grads():
        others(GROUP, me_row, lambda j: finish(row_copy(j, j)))
        others(GROUP, me_col, lambda j: finish(col_copy(j, j)))
        row_lse = merged(rowst)
        col_lse = merged(colst)
        row_out[...] = pltpu.roll(row_lse, LANES - 4 * me_row, 1)[:, 0:4]
        col_out[...] = pltpu.roll(col_lse, LANES - 8 * z, 1)[:, 0:8]
        up = lax.broadcasted_iota(jnp.int32, (64, LANES), 0)
        across = lax.broadcasted_iota(jnp.int32, (64, LANES), 1)
        inside = across < 64
        a = logit[...]
        pair = image_ids(up) == text_ids(across)
        d = jnp.exp(a - upright(row_lse)) + jnp.exp(a - col_lse) - jnp.where(pair, 2.0, 0.0)
        d = jnp.where(inside, d, 0.0).astype(BF16)
        b = logit_t[...]
        pair_t = text_ids(up) == image_ids(across)
        dt = jnp.exp(b - row_lse) + jnp.exp(b - upright(col_lse)) - jnp.where(pair_t, 2.0, 0.0)
        dt = jnp.where(inside, dt, 0.0).astype(BF16)
        gi = 100.0 * jnp.dot(d, txt2[...], preferred_element_type=F32)
        gt = 100.0 * jnp.dot(dt, img2[...], preferred_element_type=F32)
        for j in range(GROUP):
            gi_send[j] = gi[4 * j:4 * j + 4]
        for j in range(N_Z):
            gt_send[j] = gt[8 * j:8 * j + 8]
        gi_recv[me_row] = gi_send[me_row]
        gt_recv[z] = gt_send[z]
        others(GROUP, me_row, lambda j: gi_copy(me_row, j).start())
        others(N_Z, z, lambda j: gt_copy(z, j).start())

    def loss_sums():
        others(GROUP, me_row, lambda j: finish(gi_copy(j, j)))
        others(N_Z, z, lambda j: finish(gt_copy(j, j)))
        grad_image[...] = functools.reduce(jnp.add, [gi_recv[j] for j in range(GROUP)])
        gt_half[...] = functools.reduce(jnp.add, [gt_recv[j] for j in range(N_Z)])
        half_copy.start()

    def strip_copy(n):
        i, s = lax.div(n, STRIPS), lax.rem(n, STRIPS)
        rows = pl.ds(pl.multiple_of(s * POS, POS), POS)
        return remote(outbuf.at[i, rows], src.at[i, rows], strip_send.at[n], strip_recv.at[n], (1, dp))

    def store_copy(n):
        i, s = lax.div(n, STRIPS), lax.rem(n, STRIPS)
        rows = pl.ds(pl.multiple_of(s * POS, POS), POS)
        return pltpu.make_async_copy(outbuf.at[i, rows], out.at[0, i, rows], store_sem.at[n])

    def arrive(n):
        i, s = lax.div(n, STRIPS), lax.rem(n, STRIPS)

        @pl.when(sec == 1)
        def _():
            strip_copy(n).wait_recv()
        v = src[i, pl.ds(pl.multiple_of(s * POS, POS), POS)].astype(F32)
        for c in range(tiles):
            xpad[i, c, pl.ds(3 + STRIP * s, STRIP), LEFT:LEFT + SIDE] = (
                v[:, c * LANES:(c + 1) * LANES].reshape(STRIP, SIDE, LANES))

    def block(i, s):
        half = 4

        def convolve(n, carry):
            c, h = lax.div(n, STRIP // half), lax.rem(n, STRIP // half)
            acc = jnp.zeros((half, 4, 8, LANES), F32)
            for dw in range(7):
                start = LEFT - 3 + dw
                xs = xpad[i, c, pl.ds(STRIP * s + half * h, half + 6), start:start + SIDE]
                xs = xs.reshape(half + 6, 4, 8, LANES)
                for dh in range(7):
                    acc = acc + xs[dh:dh + half] * taps[c, dh * 7 + dw]
            rows = pl.ds(pl.multiple_of(h * half * SIDE, half * SIDE), half * SIDE)
            conv[c, rows] = acc.reshape(half * SIDE, LANES)
            return carry

        lax.fori_loop(0, tiles * (STRIP // half), convolve, 0)

        def part(ref, c):
            return ref[0:1, c * LANES:(c + 1) * LANES].astype(F32)

        for q in range(4):
            rows = slice(q * POS // 4, (q + 1) * POS // 4)
            v = [conv[c, rows] + part(dw_bias, c) for c in range(tiles)]
            mean = jnp.sum(functools.reduce(jnp.add, v), axis=1, keepdims=True) * (1.0 / channels)
            v = [a - mean for a in v]
            var = jnp.sum(functools.reduce(jnp.add, [a * a for a in v]), axis=1, keepdims=True) * (1.0 / channels)
            scale = lax.rsqrt(var + 1e-06)
            for c in range(tiles):
                normed[rows, c * LANES:(c + 1) * LANES] = (
                    v[c] * scale * part(norm_gain, c) + part(norm_bias, c)).astype(BF16)

        for n in range(hidden // CHUNK):
            cols = slice(n * CHUNK, (n + 1) * CHUNK)
            h = jnp.dot(normed[...], w_in_v[:, cols], preferred_element_type=F32)
            h = h + b_in[0:1, cols].astype(F32)
            g = (0.5 * h * (1.0 + lax.erf(h * 0.7071067811865476))).astype(BF16)
            p = jnp.dot(g, w_out_v[cols], preferred_element_type=F32)
            if n == 0:
                branch[...] = p
            else:
                branch[...] += p

        for c in range(tiles):
            cols = slice(c * LANES, (c + 1) * LANES)
            x = xpad[i, c, pl.ds(3 + STRIP * s, STRIP), LEFT:LEFT + SIDE].reshape(POS, LANES)
            r = x + part(layer_scale, c) * (branch[:, cols] + part(b_out, c))
            outbuf[i, pl.ds(pl.multiple_of(s * POS, POS), POS), cols] = r.astype(BF16)

    @pl.when(sec == 0)
    def _():
        load_x.wait()
    load_a.wait()
    load_b.wait()

    def step(k, carry):
        i, s = lax.div(k, STRIPS), lax.rem(k, STRIPS)

        @pl.when(k == 2 - 2 * sec)
        def _():
            loss_logits()

        @pl.when(k == 4 - 3 * sec)
        def _():
            loss_grads()

        @pl.when(k == 6 - 3 * sec)
        def _():
            loss_sums()

        @pl.when(s == 0)
        def _():
            arrive(k)

        @pl.when(s < STRIPS - 1)
        def _():
            arrive(k + 1)
        block(i, s)

        @pl.when(sec == 0)
        def _():
            strip_copy(k).start()
        store_copy(k).start()
        return carry

    lax.fori_loop(0, total, step, 0)

    half_copy.wait_send()
    half_copy.wait_recv()
    grad_text[...] = gt_half[...] + gt_other[...]

    def drain(n, carry):
        store_copy(n).wait()

        @pl.when(sec == 0)
        def _():
            strip_copy(n).wait_send()
        return carry

    lax.fori_loop(0, total, drain, 0)


def local(images, dw_kernel, dw_bias, norm_gain, norm_bias, w_in, b_in, w_out, b_out, layer_scale,
          image_embed, text_embed):
    micro, positions, channels = images.shape
    hidden = w_in.shape[2]
    width = image_embed.shape[1]
    rows, shard = image_embed.shape[0], text_embed.shape[0]
    tiles = channels // LANES
    total = micro * STRIPS
    vmem = pl.BlockSpec(memory_space=pltpu.VMEM)
    hbm = pl.BlockSpec(memory_space=pl.ANY)
    dma = pltpu.SemaphoreType.DMA
    section_out, row_lse, col_lse, grad_image, grad_text = pl.pallas_call(
        kernel,
        out_shape=(
            jax.ShapeDtypeStruct((1,) + images.shape, BF16),
            jax.ShapeDtypeStruct((1, rows), F32),
            jax.ShapeDtypeStruct((1, shard), F32),
            jax.ShapeDtypeStruct((rows, width), F32),
            jax.ShapeDtypeStruct((shard, width), F32),
        ),
        in_specs=[hbm, vmem, vmem, vmem, vmem, hbm, vmem, hbm, vmem, vmem, vmem, vmem],
        out_specs=(hbm, vmem, vmem, vmem, vmem),
        scratch_shapes=[
            pltpu.VMEM(images.shape, BF16),
            pltpu.VMEM(images.shape, BF16),
            pltpu.VMEM((micro, tiles, SIDE + 6, LEFT + SIDE + 8, LANES), F32),
            pltpu.VMEM((tiles, 49, 8, LANES), F32),
            pltpu.VMEM((tiles, POS, LANES), F32),
            pltpu.VMEM((POS, channels), BF16),
            pltpu.VMEM((POS, channels), F32),
            pltpu.VMEM((channels, hidden), BF16),
            pltpu.VMEM((hidden, channels), BF16),
            pltpu.VMEM((GROUP, rows, width), BF16),
            pltpu.VMEM((N_Z, shard, width), BF16),
            pltpu.VMEM((64, width), F32),
            pltpu.VMEM((128, width), BF16),
            pltpu.VMEM((128, width), BF16),
            pltpu.VMEM((64, LANES), F32),
            pltpu.VMEM((64, LANES), F32),
            pltpu.VMEM((GROUP, 1, LANES), F32),
            pltpu.VMEM((GROUP, 1, LANES), F32),
            pltpu.VMEM((GROUP, rows, width), F32),
            pltpu.VMEM((GROUP, rows, width), F32),
            pltpu.VMEM((N_Z, shard, width), F32),
            pltpu.VMEM((N_Z, shard, width), F32),
            pltpu.VMEM((shard, width), F32),
            pltpu.VMEM((shard, width), F32),
            dma((3,)), dma((total,)), dma((total,)), dma((total,)),
            dma((GROUP,)), dma((GROUP,)), dma((N_Z,)), dma((N_Z,)),
            dma((GROUP,)), dma((GROUP,)), dma((GROUP,)), dma((GROUP,)),
            dma((GROUP,)), dma((GROUP,)), dma((N_Z,)), dma((N_Z,)),
            dma, dma,
        ],
        compiler_params=pltpu.CompilerParams(
            collective_id=0, has_side_effects=True, vmem_limit_bytes=56 * 1024 * 1024),
        name="sections_and_loss",
    )(images, dw_kernel, dw_bias, norm_gain, norm_bias, w_in, b_in, w_out, b_out, layer_scale,
      image_embed, text_embed)
    return (section_out, row_lse.reshape(rows), col_lse.reshape(shard), grad_image, grad_text)


def solution(mesh):
    in_specs = (
        P("dp", None, None),
        P("pipe", None, None),
        P("pipe", None),
        P("pipe", None),
        P("pipe", None),
        P("pipe", None, None),
        P("pipe", None),
        P("pipe", None, None),
        P("pipe", None),
        P("pipe", None),
        P(("pipe", "dp"), None),
        P("dp", None),
    )
    out_specs = (
        P("pipe", "dp", None, None),
        P(("pipe", "dp")),
        P("dp"),
        P(("pipe", "dp"), None),
        P("dp", None),
    )
    return jax.shard_map(local, mesh=mesh, in_specs=in_specs, out_specs=out_specs, check_vma=False)
```

```python
import functools

import jax
import jax.numpy as jnp
from jax import lax
from jax.experimental import pallas as pl
from jax.experimental.pallas import tpu as pltpu
from jax.sharding import PartitionSpec as P

MESH = pl.DeviceIdType.MESH
F32 = jnp.float32
BF16 = jnp.bfloat16

N_Z, N_Y = 8, 4
GROUP = 16
SIDE = 32
LANES = 128
STRIP = 4
STRIPS = SIDE // STRIP
POS = STRIP * SIDE
LEFT = 8
CHUNK = 256


def kernel(
    images, dw_kernel, dw_bias, norm_gain, norm_bias, w_in, b_in, w_out, b_out, layer_scale,
    image_embed, text_embed,
    out, row_out, col_out, grad_image, grad_text,
    src, outbuf, xpad, taps, conv, normed, branch, w_in_v, w_out_v,
    imgbuf, txtbuf, imgf, img2, txt2, logit, logit_t, rowst, colst,
    gi_send, gi_recv, gt_send, gt_recv, gt_half, gt_other,
    load_sem, store_sem, strip_send, strip_recv, img_send, img_recv, txt_send, txt_recv,
    row_send, row_recv, col_send, col_recv, gis_sem, gir_sem, gts_sem, gtr_sem, half_send, half_recv,
):
    sec = lax.axis_index("pipe")
    dp = lax.axis_index("dp")
    core = lax.rem(dp, 2)
    y = lax.rem(lax.div(dp, 2), N_Y)
    z = lax.rem(lax.div(dp, 2 * N_Y), N_Z)
    x_lo = lax.div(dp, 2 * N_Y * N_Z)
    me_row = x_lo * 8 + y * 2 + core
    me_col = sec * N_Z + z
    micro = src.shape[0]
    channels = src.shape[2]
    tiles = channels // LANES
    hidden = w_in_v.shape[1]
    total = micro * STRIPS

    def row_peer(j):
        return (sec, ((lax.div(j, 8) * N_Z + z) * N_Y + lax.rem(lax.div(j, 2), N_Y)) * 2 + lax.rem(j, 2))

    def col_peer(j):
        return (lax.div(j, N_Z), ((x_lo * N_Z + lax.rem(j, N_Z)) * N_Y + y) * 2 + core)

    def text_peer(j):
        return (sec, ((x_lo * N_Z + j) * N_Y + y) * 2 + core)

    partner = (1 - sec, dp)

    def remote(source, target, send, recv, device):
        return pltpu.make_async_remote_copy(
            src_ref=source, dst_ref=target, send_sem=send, recv_sem=recv,
            device_id=device, device_id_type=MESH,
        )

    def others(count, me, act):
        def one(j, carry):
            @pl.when(j != me)
            def _():
                act(j)
            return carry
        lax.fori_loop(0, count, one, 0)

    load_x = pltpu.make_async_copy(images, src, load_sem.at[0])
    load_a = pltpu.make_async_copy(w_in.at[0], w_in_v, load_sem.at[1])
    load_b = pltpu.make_async_copy(w_out.at[0], w_out_v, load_sem.at[2])

    @pl.when(sec == 0)
    def _():
        load_x.start()
    load_a.start()
    load_b.start()

    barrier = pltpu.get_barrier_semaphore()
    others(GROUP, me_row, lambda j: pl.semaphore_signal(
        barrier, inc=1, device_id=row_peer(j), device_id_type=MESH))
    others(GROUP, me_col, lambda j: pl.semaphore_signal(
        barrier, inc=1, device_id=col_peer(j), device_id_type=MESH))

    def unit(values):
        wide = values.astype(F32)
        return (wide * lax.rsqrt(jnp.sum(wide * wide, axis=1, keepdims=True) + 1e-06)).astype(BF16)

    imgbuf[me_row] = unit(image_embed[...])
    txtbuf[z] = unit(text_embed[...])

    xpad[:, :, 0:3] = jnp.zeros(xpad.shape[:2] + (3,) + xpad.shape[3:], F32)
    xpad[:, :, SIDE + 3:SIDE + 6] = jnp.zeros(xpad.shape[:2] + (3,) + xpad.shape[3:], F32)
    xpad[:, :, :, 0:LEFT] = jnp.zeros(xpad.shape[:3] + (LEFT, LANES), F32)
    xpad[:, :, :, LEFT + SIDE:] = jnp.zeros(xpad.shape[:3] + (8, LANES), F32)
    kv = dw_kernel[0].astype(F32)
    for c in range(tiles):
        for t in range(49):
            taps[c, t] = jnp.broadcast_to(kv[t:t + 1, c * LANES:(c + 1) * LANES], (8, LANES))

    pl.semaphore_wait(barrier, 2 * (GROUP - 1))

    def img_copy(slot, j):
        return remote(imgbuf.at[slot], imgbuf.at[slot], img_send.at[j], img_recv.at[slot], row_peer(j))

    def txt_copy(slot, j):
        return remote(txtbuf.at[slot], txtbuf.at[slot], txt_send.at[j], txt_recv.at[slot], text_peer(j))

    def row_copy(slot, j):
        return remote(rowst.at[slot], rowst.at[slot], row_send.at[j], row_recv.at[slot], row_peer(j))

    def col_copy(slot, j):
        return remote(colst.at[slot], colst.at[slot], col_send.at[j], col_recv.at[slot], col_peer(j))

    def gi_copy(slot, j):
        return remote(gi_send.at[j], gi_recv.at[slot], gis_sem.at[j], gir_sem.at[slot], row_peer(j))

    def gt_copy(slot, j):
        return remote(gt_send.at[j], gt_recv.at[slot], gts_sem.at[j], gtr_sem.at[slot], text_peer(j))

    half_copy = remote(gt_half, gt_other, half_send, half_recv, partner)

    others(GROUP, me_row, lambda j: img_copy(me_row, j).start())
    others(N_Z, z, lambda j: txt_copy(z, j).start())

    def finish(copy):
        copy.wait_send()
        copy.wait_recv()

    lane = lax.broadcasted_iota(jnp.int32, (1, LANES), 1)
    low = lane < 64

    def loss_logits():
        others(GROUP, me_row, lambda j: finish(img_copy(j, j)))
        others(N_Z, z, lambda j: finish(txt_copy(j, j)))
        for j in range(GROUP):
            imgf[4 * j:4 * j + 4] = imgbuf[j].astype(F32)
        img = imgf[...].astype(BF16)
        img2[0:64] = img
        img2[64:128] = img
        for j in range(N_Z):
            imgf[8 * j:8 * j + 8] = txtbuf[j].astype(F32)
        txt = imgf[...].astype(BF16)
        txt2[0:64] = txt
        txt2[64:128] = txt
        dims = (((1,), (1,)), ((), ()))
        a = 100.0 * lax.dot_general(img2[0:64], txt2[...], dims, preferred_element_type=F32)
        b = 100.0 * lax.dot_general(txt2[0:64], img2[...], dims, preferred_element_type=F32)
        logit[...] = a
        logit_t[...] = b

        def stats(values):
            top = jnp.max(values, axis=0, keepdims=True)
            return jnp.where(low, top, jnp.sum(jnp.exp(values - top), axis=0, keepdims=True))

        colst[me_col] = stats(a)
        rowst[me_row] = stats(b)
        others(GROUP, me_row, lambda j: row_copy(me_row, j).start())
        others(GROUP, me_col, lambda j: col_copy(me_col, j).start())

    def merged(ref):
        parts = [ref[j] for j in range(GROUP)]
        top = functools.reduce(jnp.maximum, parts)
        add = functools.reduce(
            jnp.add, [pltpu.roll(p, 64, 1) * jnp.exp(jnp.where(low, p - top, 0.0)) for p in parts])
        lse = top + jnp.log(jnp.where(low, add, 1.0))
        return jnp.where(low, lse, pltpu.roll(lse, 64, 1))

    def upright(row):
        here = lax.broadcasted_iota(jnp.int32, (64, LANES), 0) == lax.broadcasted_iota(jnp.int32, (64, LANES), 1)
        return jnp.sum(jnp.where(here, row, 0.0), axis=1, keepdims=True)

    def image_ids(r):
        j = r >> 2
        peer = (((j >> 3) * N_Z + z) * N_Y + ((j >> 1) & 3)) * 2 + (j & 1)
        return (sec * 128 + peer) * 4 + (r & 3)

    def text_ids(r):
        return (((x_lo * N_Z + (r >> 3)) * N_Y + y) * 2 + core) * 8 + (r & 7)

    def loss_grads():
        others(GROUP, me_row, lambda j: finish(row_copy(j, j)))
        others(GROUP, me_col, lambda j: finish(col_copy(j, j)))
        row_lse = merged(rowst)
        col_lse = merged(colst)
        row_out[...] = pltpu.roll(row_lse, LANES - 4 * me_row, 1)[:, 0:4]
        col_out[...] = pltpu.roll(col_lse, LANES - 8 * z, 1)[:, 0:8]
        up = lax.broadcasted_iota(jnp.int32, (64, LANES), 0)
        across = lax.broadcasted_iota(jnp.int32, (64, LANES), 1)
        inside = across < 64
        a = logit[...]
        pair = image_ids(up) == text_ids(across)
        d = jnp.exp(a - upright(row_lse)) + jnp.exp(a - col_lse) - jnp.where(pair, 2.0, 0.0)
        d = jnp.where(inside, d, 0.0).astype(BF16)
        b = logit_t[...]
        pair_t = text_ids(up) == image_ids(across)
        dt = jnp.exp(b - row_lse) + jnp.exp(b - upright(col_lse)) - jnp.where(pair_t, 2.0, 0.0)
        dt = jnp.where(inside, dt, 0.0).astype(BF16)
        gi = 100.0 * jnp.dot(d, txt2[...], preferred_element_type=F32)
        gt = 100.0 * jnp.dot(dt, img2[...], preferred_element_type=F32)
        for j in range(GROUP):
            gi_send[j] = gi[4 * j:4 * j + 4]
        for j in range(N_Z):
            gt_send[j] = gt[8 * j:8 * j + 8]
        gi_recv[me_row] = gi_send[me_row]
        gt_recv[z] = gt_send[z]
        others(GROUP, me_row, lambda j: gi_copy(me_row, j).start())
        others(N_Z, z, lambda j: gt_copy(z, j).start())

    def loss_sums():
        others(GROUP, me_row, lambda j: finish(gi_copy(j, j)))
        others(N_Z, z, lambda j: finish(gt_copy(j, j)))
        grad_image[...] = functools.reduce(jnp.add, [gi_recv[j] for j in range(GROUP)])
        gt_half[...] = functools.reduce(jnp.add, [gt_recv[j] for j in range(N_Z)])
        half_copy.start()

    def strip_copy(n):
        i, s = lax.div(n, STRIPS), lax.rem(n, STRIPS)
        rows = pl.ds(pl.multiple_of(s * POS, POS), POS)
        return remote(outbuf.at[i, rows], src.at[i, rows], strip_send.at[n], strip_recv.at[n], (1, dp))

    def store_copy(n):
        i, s = lax.div(n, STRIPS), lax.rem(n, STRIPS)
        rows = pl.ds(pl.multiple_of(s * POS, POS), POS)
        return pltpu.make_async_copy(outbuf.at[i, rows], out.at[0, i, rows], store_sem.at[n])

    def arrive(n):
        i, s = lax.div(n, STRIPS), lax.rem(n, STRIPS)

        @pl.when(sec == 1)
        def _():
            strip_copy(n).wait_recv()
        v = src[i, pl.ds(pl.multiple_of(s * POS, POS), POS)].astype(F32)
        for c in range(tiles):
            xpad[i, c, pl.ds(3 + STRIP * s, STRIP), LEFT:LEFT + SIDE] = (
                v[:, c * LANES:(c + 1) * LANES].reshape(STRIP, SIDE, LANES))

    def block(i, s):
        half = 4

        def convolve(n, carry):
            c, h = lax.div(n, STRIP // half), lax.rem(n, STRIP // half)
            acc = jnp.zeros((half, 4, 8, LANES), F32)
            for dw in range(7):
                start = LEFT - 3 + dw
                xs = xpad[i, c, pl.ds(STRIP * s + half * h, half + 6), start:start + SIDE]
                xs = xs.reshape(half + 6, 4, 8, LANES)
                for dh in range(7):
                    acc = acc + xs[dh:dh + half] * taps[c, dh * 7 + dw]
            rows = pl.ds(pl.multiple_of(h * half * SIDE, half * SIDE), half * SIDE)
            conv[c, rows] = acc.reshape(half * SIDE, LANES)
            return carry

        lax.fori_loop(0, tiles * (STRIP // half), convolve, 0)

        def part(ref, c):
            return ref[0:1, c * LANES:(c + 1) * LANES].astype(F32)

        for q in range(4):
            rows = slice(q * POS // 4, (q + 1) * POS // 4)
            v = [conv[c, rows] + part(dw_bias, c) for c in range(tiles)]
            mean = jnp.sum(functools.reduce(jnp.add, v), axis=1, keepdims=True) * (1.0 / channels)
            v = [a - mean for a in v]
            var = jnp.sum(functools.reduce(jnp.add, [a * a for a in v]), axis=1, keepdims=True) * (1.0 / channels)
            scale = lax.rsqrt(var + 1e-06)
            for c in range(tiles):
                normed[rows, c * LANES:(c + 1) * LANES] = (
                    v[c] * scale * part(norm_gain, c) + part(norm_bias, c)).astype(BF16)

        for n in range(hidden // CHUNK):
            cols = slice(n * CHUNK, (n + 1) * CHUNK)
            h = jnp.dot(normed[...], w_in_v[:, cols], preferred_element_type=F32)
            h = h + b_in[0:1, cols].astype(F32)
            g = (0.5 * h * (1.0 + lax.erf(h * 0.7071067811865476))).astype(BF16)
            p = jnp.dot(g, w_out_v[cols], preferred_element_type=F32)
            if n == 0:
                branch[...] = p
            else:
                branch[...] += p

        for c in range(tiles):
            cols = slice(c * LANES, (c + 1) * LANES)
            x = xpad[i, c, pl.ds(3 + STRIP * s, STRIP), LEFT:LEFT + SIDE].reshape(POS, LANES)
            r = x + part(layer_scale, c) * (branch[:, cols] + part(b_out, c))
            outbuf[i, pl.ds(pl.multiple_of(s * POS, POS), POS), cols] = r.astype(BF16)

    @pl.when(sec == 0)
    def _():
        load_x.wait()
    load_a.wait()
    load_b.wait()

    def strip(k):
        i, s = lax.div(k, STRIPS), lax.rem(k, STRIPS)

        @pl.when(s == 0)
        def _():
            arrive(k)

        @pl.when(s < STRIPS - 1)
        def _():
            arrive(k + 1)
        block(i, s)

        @pl.when(sec == 0)
        def _():
            strip_copy(k).start()
        store_copy(k).start()

    def step(k, carry):
        @pl.when(k == 1 - sec)
        def _():
            loss_logits()

        @pl.when(k == total * (1 - sec))
        def _():
            loss_grads()
            loss_sums()

        @pl.when(k < total)
        def _():
            strip(k)
        return carry

    lax.fori_loop(0, total + 1, step, 0)

    half_copy.wait_send()
    half_copy.wait_recv()
    grad_text[...] = gt_half[...] + gt_other[...]

    def drain(n, carry):
        store_copy(n).wait()

        @pl.when(sec == 0)
        def _():
            strip_copy(n).wait_send()
        return carry

    lax.fori_loop(0, total, drain, 0)


def local(images, dw_kernel, dw_bias, norm_gain, norm_bias, w_in, b_in, w_out, b_out, layer_scale,
          image_embed, text_embed):
    micro, positions, channels = images.shape
    hidden = w_in.shape[2]
    width = image_embed.shape[1]
    rows, shard = image_embed.shape[0], text_embed.shape[0]
    tiles = channels // LANES
    total = micro * STRIPS
    vmem = pl.BlockSpec(memory_space=pltpu.VMEM)
    hbm = pl.BlockSpec(memory_space=pl.ANY)
    dma = pltpu.SemaphoreType.DMA
    section_out, row_lse, col_lse, grad_image, grad_text = pl.pallas_call(
        kernel,
        out_shape=(
            jax.ShapeDtypeStruct((1,) + images.shape, BF16),
            jax.ShapeDtypeStruct((1, rows), F32),
            jax.ShapeDtypeStruct((1, shard), F32),
            jax.ShapeDtypeStruct((rows, width), F32),
            jax.ShapeDtypeStruct((shard, width), F32),
        ),
        in_specs=[hbm, vmem, vmem, vmem, vmem, hbm, vmem, hbm, vmem, vmem, vmem, vmem],
        out_specs=(hbm, vmem, vmem, vmem, vmem),
        scratch_shapes=[
            pltpu.VMEM(images.shape, BF16),
            pltpu.VMEM(images.shape, BF16),
            pltpu.VMEM((micro, tiles, SIDE + 6, LEFT + SIDE + 8, LANES), F32),
            pltpu.VMEM((tiles, 49, 8, LANES), F32),
            pltpu.VMEM((tiles, POS, LANES), F32),
            pltpu.VMEM((POS, channels), BF16),
            pltpu.VMEM((POS, channels), F32),
            pltpu.VMEM((channels, hidden), BF16),
            pltpu.VMEM((hidden, channels), BF16),
            pltpu.VMEM((GROUP, rows, width), BF16),
            pltpu.VMEM((N_Z, shard, width), BF16),
            pltpu.VMEM((64, width), F32),
            pltpu.VMEM((128, width), BF16),
            pltpu.VMEM((128, width), BF16),
            pltpu.VMEM((64, LANES), F32),
            pltpu.VMEM((64, LANES), F32),
            pltpu.VMEM((GROUP, 1, LANES), F32),
            pltpu.VMEM((GROUP, 1, LANES), F32),
            pltpu.VMEM((GROUP, rows, width), F32),
            pltpu.VMEM((GROUP, rows, width), F32),
            pltpu.VMEM((N_Z, shard, width), F32),
            pltpu.VMEM((N_Z, shard, width), F32),
            pltpu.VMEM((shard, width), F32),
            pltpu.VMEM((shard, width), F32),
            dma((3,)), dma((total,)), dma((total,)), dma((total,)),
            dma((GROUP,)), dma((GROUP,)), dma((N_Z,)), dma((N_Z,)),
            dma((GROUP,)), dma((GROUP,)), dma((GROUP,)), dma((GROUP,)),
            dma((GROUP,)), dma((GROUP,)), dma((N_Z,)), dma((N_Z,)),
            dma, dma,
        ],
        compiler_params=pltpu.CompilerParams(
            collective_id=0, has_side_effects=True, vmem_limit_bytes=56 * 1024 * 1024),
        name="sections_and_loss",
    )(images, dw_kernel, dw_bias, norm_gain, norm_bias, w_in, b_in, w_out, b_out, layer_scale,
      image_embed, text_embed)
    return (section_out, row_lse.reshape(rows), col_lse.reshape(shard), grad_image, grad_text)


def solution(mesh):
    in_specs = (
        P("dp", None, None),
        P("pipe", None, None),
        P("pipe", None),
        P("pipe", None),
        P("pipe", None),
        P("pipe", None, None),
        P("pipe", None),
        P("pipe", None, None),
        P("pipe", None),
        P("pipe", None),
        P(("pipe", "dp"), None),
        P("dp", None),
    )
    out_specs = (
        P("pipe", "dp", None, None),
        P(("pipe", "dp")),
        P("dp"),
        P(("pipe", "dp"), None),
        P("dp", None),
    )
    return jax.shard_map(local, mesh=mesh, in_specs=in_specs, out_specs=out_specs, check_vma=False)
```

```python
import functools

import jax
import jax.numpy as jnp
from jax import lax
from jax.experimental import pallas as pl
from jax.experimental.pallas import tpu as pltpu
from jax.sharding import PartitionSpec as P

MESH = pl.DeviceIdType.MESH
F32 = jnp.float32
BF16 = jnp.bfloat16

N_Z, N_Y = 8, 4
GROUP = 16
SIDE = 32
LANES = 128
STRIP = 8
STRIPS = SIDE // STRIP
POS = STRIP * SIDE
LEFT = 8
CHUNK = 256


def kernel(
    images, dw_kernel, dw_bias, norm_gain, norm_bias, w_in, b_in, w_out, b_out, layer_scale,
    image_embed, text_embed,
    out, row_out, col_out, grad_image, grad_text,
    src, outbuf, xpad, taps, conv, normed, branch, w_in_v, w_out_v,
    imgbuf, txtbuf, imgf, img2, txt2, logit, logit_t, rowst, colst,
    gi_send, gi_recv, gt_send, gt_recv, gt_half, gt_other,
    load_sem, store_sem, strip_send, strip_recv, img_send, img_recv, txt_send, txt_recv,
    row_send, row_recv, col_send, col_recv, gis_sem, gir_sem, gts_sem, gtr_sem, half_send, half_recv,
):
    sec = lax.axis_index("pipe")
    dp = lax.axis_index("dp")
    core = lax.rem(dp, 2)
    y = lax.rem(lax.div(dp, 2), N_Y)
    z = lax.rem(lax.div(dp, 2 * N_Y), N_Z)
    x_lo = lax.div(dp, 2 * N_Y * N_Z)
    me_row = x_lo * 8 + y * 2 + core
    me_col = sec * N_Z + z
    micro = src.shape[0]
    channels = src.shape[2]
    tiles = channels // LANES
    hidden = w_in_v.shape[1]
    total = micro * STRIPS

    def row_peer(j):
        return (sec, ((lax.div(j, 8) * N_Z + z) * N_Y + lax.rem(lax.div(j, 2), N_Y)) * 2 + lax.rem(j, 2))

    def col_peer(j):
        return (lax.div(j, N_Z), ((x_lo * N_Z + lax.rem(j, N_Z)) * N_Y + y) * 2 + core)

    def text_peer(j):
        return (sec, ((x_lo * N_Z + j) * N_Y + y) * 2 + core)

    partner = (1 - sec, dp)

    def remote(source, target, send, recv, device):
        return pltpu.make_async_remote_copy(
            src_ref=source, dst_ref=target, send_sem=send, recv_sem=recv,
            device_id=device, device_id_type=MESH,
        )

    def others(count, me, act):
        def one(j, carry):
            @pl.when(j != me)
            def _():
                act(j)
            return carry
        lax.fori_loop(0, count, one, 0)

    load_x = pltpu.make_async_copy(images, src, load_sem.at[0])
    load_a = pltpu.make_async_copy(w_in.at[0], w_in_v, load_sem.at[1])
    load_b = pltpu.make_async_copy(w_out.at[0], w_out_v, load_sem.at[2])

    @pl.when(sec == 0)
    def _():
        load_x.start()
    load_a.start()
    load_b.start()

    barrier = pltpu.get_barrier_semaphore()
    others(GROUP, me_row, lambda j: pl.semaphore_signal(
        barrier, inc=1, device_id=row_peer(j), device_id_type=MESH))
    others(GROUP, me_col, lambda j: pl.semaphore_signal(
        barrier, inc=1, device_id=col_peer(j), device_id_type=MESH))

    def unit(values):
        wide = values.astype(F32)
        return (wide * lax.rsqrt(jnp.sum(wide * wide, axis=1, keepdims=True) + 1e-06)).astype(BF16)

    imgbuf[me_row] = unit(image_embed[...])
    txtbuf[z] = unit(text_embed[...])

    xpad[:, :, 0:3] = jnp.zeros(xpad.shape[:2] + (3,) + xpad.shape[3:], F32)
    xpad[:, :, SIDE + 3:SIDE + 6] = jnp.zeros(xpad.shape[:2] + (3,) + xpad.shape[3:], F32)
    xpad[:, :, :, 0:LEFT] = jnp.zeros(xpad.shape[:3] + (LEFT, LANES), F32)
    xpad[:, :, :, LEFT + SIDE:] = jnp.zeros(xpad.shape[:3] + (8, LANES), F32)
    kv = dw_kernel[0].astype(F32)
    for c in range(tiles):
        for t in range(49):
            taps[c, t] = jnp.broadcast_to(kv[t:t + 1, c * LANES:(c + 1) * LANES], (8, LANES))

    pl.semaphore_wait(barrier, 2 * (GROUP - 1))

    def img_copy(slot, j):
        return remote(imgbuf.at[slot], imgbuf.at[slot], img_send.at[j], img_recv.at[slot], row_peer(j))

    def txt_copy(slot, j):
        return remote(txtbuf.at[slot], txtbuf.at[slot], txt_send.at[j], txt_recv.at[slot], text_peer(j))

    def row_copy(slot, j):
        return remote(rowst.at[slot], rowst.at[slot], row_send.at[j], row_recv.at[slot], row_peer(j))

    def col_copy(slot, j):
        return remote(colst.at[slot], colst.at[slot], col_send.at[j], col_recv.at[slot], col_peer(j))

    def gi_copy(slot, j):
        return remote(gi_send.at[j], gi_recv.at[slot], gis_sem.at[j], gir_sem.at[slot], row_peer(j))

    def gt_copy(slot, j):
        return remote(gt_send.at[j], gt_recv.at[slot], gts_sem.at[j], gtr_sem.at[slot], text_peer(j))

    half_copy = remote(gt_half, gt_other, half_send, half_recv, partner)

    others(GROUP, me_row, lambda j: img_copy(me_row, j).start())
    others(N_Z, z, lambda j: txt_copy(z, j).start())

    def finish(copy):
        copy.wait_send()
        copy.wait_recv()

    lane = lax.broadcasted_iota(jnp.int32, (1, LANES), 1)
    low = lane < 64

    def loss_logits():
        others(GROUP, me_row, lambda j: finish(img_copy(j, j)))
        others(N_Z, z, lambda j: finish(txt_copy(j, j)))
        for j in range(GROUP):
            imgf[4 * j:4 * j + 4] = imgbuf[j].astype(F32)
        img = imgf[...].astype(BF16)
        img2[0:64] = img
        img2[64:128] = img
        for j in range(N_Z):
            imgf[8 * j:8 * j + 8] = txtbuf[j].astype(F32)
        txt = imgf[...].astype(BF16)
        txt2[0:64] = txt
        txt2[64:128] = txt
        dims = (((1,), (1,)), ((), ()))
        a = 100.0 * lax.dot_general(img2[0:64], txt2[...], dims, preferred_element_type=F32)
        b = 100.0 * lax.dot_general(txt2[0:64], img2[...], dims, preferred_element_type=F32)
        logit[...] = a
        logit_t[...] = b

        def stats(values):
            top = jnp.max(values, axis=0, keepdims=True)
            return jnp.where(low, top, jnp.sum(jnp.exp(values - top), axis=0, keepdims=True))

        colst[me_col] = stats(a)
        rowst[me_row] = stats(b)
        others(GROUP, me_row, lambda j: row_copy(me_row, j).start())
        others(GROUP, me_col, lambda j: col_copy(me_col, j).start())

    def merged(ref):
        parts = [ref[j] for j in range(GROUP)]
        top = functools.reduce(jnp.maximum, parts)
        add = functools.reduce(
            jnp.add, [pltpu.roll(p, 64, 1) * jnp.exp(jnp.where(low, p - top, 0.0)) for p in parts])
        lse = top + jnp.log(jnp.where(low, add, 1.0))
        return jnp.where(low, lse, pltpu.roll(lse, 64, 1))

    def upright(row):
        here = lax.broadcasted_iota(jnp.int32, (64, LANES), 0) == lax.broadcasted_iota(jnp.int32, (64, LANES), 1)
        return jnp.sum(jnp.where(here, row, 0.0), axis=1, keepdims=True)

    def image_ids(r):
        j = r >> 2
        peer = (((j >> 3) * N_Z + z) * N_Y + ((j >> 1) & 3)) * 2 + (j & 1)
        return (sec * 128 + peer) * 4 + (r & 3)

    def text_ids(r):
        return (((x_lo * N_Z + (r >> 3)) * N_Y + y) * 2 + core) * 8 + (r & 7)

    def loss_grads():
        others(GROUP, me_row, lambda j: finish(row_copy(j, j)))
        others(GROUP, me_col, lambda j: finish(col_copy(j, j)))
        row_lse = merged(rowst)
        col_lse = merged(colst)
        row_out[...] = pltpu.roll(row_lse, LANES - 4 * me_row, 1)[:, 0:4]
        col_out[...] = pltpu.roll(col_lse, LANES - 8 * z, 1)[:, 0:8]
        up = lax.broadcasted_iota(jnp.int32, (64, LANES), 0)
        across = lax.broadcasted_iota(jnp.int32, (64, LANES), 1)
        inside = across < 64
        a = logit[...]
        pair = image_ids(up) == text_ids(across)
        d = jnp.exp(a - upright(row_lse)) + jnp.exp(a - col_lse) - jnp.where(pair, 2.0, 0.0)
        d = jnp.where(inside, d, 0.0).astype(BF16)
        b = logit_t[...]
        pair_t = text_ids(up) == image_ids(across)
        dt = jnp.exp(b - row_lse) + jnp.exp(b - upright(col_lse)) - jnp.where(pair_t, 2.0, 0.0)
        dt = jnp.where(inside, dt, 0.0).astype(BF16)
        gi = 100.0 * jnp.dot(d, txt2[...], preferred_element_type=F32)
        gt = 100.0 * jnp.dot(dt, img2[...], preferred_element_type=F32)
        for j in range(GROUP):
            gi_send[j] = gi[4 * j:4 * j + 4]
        for j in range(N_Z):
            gt_send[j] = gt[8 * j:8 * j + 8]
        gi_recv[me_row] = gi_send[me_row]
        gt_recv[z] = gt_send[z]
        others(GROUP, me_row, lambda j: gi_copy(me_row, j).start())
        others(N_Z, z, lambda j: gt_copy(z, j).start())

    def loss_sums():
        others(GROUP, me_row, lambda j: finish(gi_copy(j, j)))
        others(N_Z, z, lambda j: finish(gt_copy(j, j)))
        grad_image[...] = functools.reduce(jnp.add, [gi_recv[j] for j in range(GROUP)])
        gt_half[...] = functools.reduce(jnp.add, [gt_recv[j] for j in range(N_Z)])
        half_copy.start()

    def strip_copy(n):
        i, s = lax.div(n, STRIPS), lax.rem(n, STRIPS)
        rows = pl.ds(pl.multiple_of(s * POS, POS), POS)
        return remote(outbuf.at[i, rows], src.at[i, rows], strip_send.at[n], strip_recv.at[n], (1, dp))

    def store_copy(n):
        i, s = lax.div(n, STRIPS), lax.rem(n, STRIPS)
        rows = pl.ds(pl.multiple_of(s * POS, POS), POS)
        return pltpu.make_async_copy(outbuf.at[i, rows], out.at[0, i, rows], store_sem.at[n])

    def arrive(n):
        i, s = lax.div(n, STRIPS), lax.rem(n, STRIPS)

        @pl.when(sec == 1)
        def _():
            strip_copy(n).wait_recv()
        v = src[i, pl.ds(pl.multiple_of(s * POS, POS), POS)].astype(F32)
        for c in range(tiles):
            xpad[i, c, pl.ds(3 + STRIP * s, STRIP), LEFT:LEFT + SIDE] = (
                v[:, c * LANES:(c + 1) * LANES].reshape(STRIP, SIDE, LANES))

    def block(i, s):
        half = 4

        def convolve(n, carry):
            c, h = lax.div(n, STRIP // half), lax.rem(n, STRIP // half)
            acc = jnp.zeros((half, 4, 8, LANES), F32)
            for dw in range(7):
                start = LEFT - 3 + dw
                xs = xpad[i, c, pl.ds(STRIP * s + half * h, half + 6), start:start + SIDE]
                xs = xs.reshape(half + 6, 4, 8, LANES)
                for dh in range(7):
                    acc = acc + xs[dh:dh + half] * taps[c, dh * 7 + dw]
            rows = pl.ds(pl.multiple_of(h * half * SIDE, half * SIDE), half * SIDE)
            conv[c, rows] = acc.reshape(half * SIDE, LANES)
            return carry

        lax.fori_loop(0, tiles * (STRIP // half), convolve, 0)

        def part(ref, c):
            return ref[0:1, c * LANES:(c + 1) * LANES].astype(F32)

        for q in range(4):
            rows = slice(q * POS // 4, (q + 1) * POS // 4)
            v = [conv[c, rows] + part(dw_bias, c) for c in range(tiles)]
            mean = jnp.sum(functools.reduce(jnp.add, v), axis=1, keepdims=True) * (1.0 / channels)
            v = [a - mean for a in v]
            var = jnp.sum(functools.reduce(jnp.add, [a * a for a in v]), axis=1, keepdims=True) * (1.0 / channels)
            scale = lax.rsqrt(var + 1e-06)
            for c in range(tiles):
                normed[rows, c * LANES:(c + 1) * LANES] = (
                    v[c] * scale * part(norm_gain, c) + part(norm_bias, c)).astype(BF16)

        for n in range(hidden // CHUNK):
            cols = slice(n * CHUNK, (n + 1) * CHUNK)
            h = jnp.dot(normed[...], w_in_v[:, cols], preferred_element_type=F32)
            h = h + b_in[0:1, cols].astype(F32)
            g = (0.5 * h * (1.0 + lax.erf(h * 0.7071067811865476))).astype(BF16)
            p = jnp.dot(g, w_out_v[cols], preferred_element_type=F32)
            if n == 0:
                branch[...] = p
            else:
                branch[...] += p

        for c in range(tiles):
            cols = slice(c * LANES, (c + 1) * LANES)
            x = xpad[i, c, pl.ds(3 + STRIP * s, STRIP), LEFT:LEFT + SIDE].reshape(POS, LANES)
            r = x + part(layer_scale, c) * (branch[:, cols] + part(b_out, c))
            outbuf[i, pl.ds(pl.multiple_of(s * POS, POS), POS), cols] = r.astype(BF16)

    @pl.when(sec == 0)
    def _():
        load_x.wait()
    load_a.wait()
    load_b.wait()

    def strip(k):
        i, s = lax.div(k, STRIPS), lax.rem(k, STRIPS)

        @pl.when(s == 0)
        def _():
            arrive(k)

        @pl.when(s < STRIPS - 1)
        def _():
            arrive(k + 1)
        block(i, s)

        @pl.when(sec == 0)
        def _():
            strip_copy(k).start()
        store_copy(k).start()

    def step(k, carry):
        @pl.when(k == 1 - sec)
        def _():
            loss_logits()

        @pl.when(k == total * (1 - sec))
        def _():
            loss_grads()
            loss_sums()

        @pl.when(k < total)
        def _():
            strip(k)
        return carry

    lax.fori_loop(0, total + 1, step, 0)

    half_copy.wait_send()
    half_copy.wait_recv()
    grad_text[...] = gt_half[...] + gt_other[...]

    def drain(n, carry):
        store_copy(n).wait()

        @pl.when(sec == 0)
        def _():
            strip_copy(n).wait_send()
        return carry

    lax.fori_loop(0, total, drain, 0)


def local(images, dw_kernel, dw_bias, norm_gain, norm_bias, w_in, b_in, w_out, b_out, layer_scale,
          image_embed, text_embed):
    micro, positions, channels = images.shape
    hidden = w_in.shape[2]
    width = image_embed.shape[1]
    rows, shard = image_embed.shape[0], text_embed.shape[0]
    tiles = channels // LANES
    total = micro * STRIPS
    vmem = pl.BlockSpec(memory_space=pltpu.VMEM)
    hbm = pl.BlockSpec(memory_space=pl.ANY)
    dma = pltpu.SemaphoreType.DMA
    section_out, row_lse, col_lse, grad_image, grad_text = pl.pallas_call(
        kernel,
        out_shape=(
            jax.ShapeDtypeStruct((1,) + images.shape, BF16),
            jax.ShapeDtypeStruct((1, rows), F32),
            jax.ShapeDtypeStruct((1, shard), F32),
            jax.ShapeDtypeStruct((rows, width), F32),
            jax.ShapeDtypeStruct((shard, width), F32),
        ),
        in_specs=[hbm, vmem, vmem, vmem, vmem, hbm, vmem, hbm, vmem, vmem, vmem, vmem],
        out_specs=(hbm, vmem, vmem, vmem, vmem),
        scratch_shapes=[
            pltpu.VMEM(images.shape, BF16),
            pltpu.VMEM(images.shape, BF16),
            pltpu.VMEM((micro, tiles, SIDE + 6, LEFT + SIDE + 8, LANES), F32),
            pltpu.VMEM((tiles, 49, 8, LANES), F32),
            pltpu.VMEM((tiles, POS, LANES), F32),
            pltpu.VMEM((POS, channels), BF16),
            pltpu.VMEM((POS, channels), F32),
            pltpu.VMEM((channels, hidden), BF16),
            pltpu.VMEM((hidden, channels), BF16),
            pltpu.VMEM((GROUP, rows, width), BF16),
            pltpu.VMEM((N_Z, shard, width), BF16),
            pltpu.VMEM((64, width), F32),
            pltpu.VMEM((128, width), BF16),
            pltpu.VMEM((128, width), BF16),
            pltpu.VMEM((64, LANES), F32),
            pltpu.VMEM((64, LANES), F32),
            pltpu.VMEM((GROUP, 1, LANES), F32),
            pltpu.VMEM((GROUP, 1, LANES), F32),
            pltpu.VMEM((GROUP, rows, width), F32),
            pltpu.VMEM((GROUP, rows, width), F32),
            pltpu.VMEM((N_Z, shard, width), F32),
            pltpu.VMEM((N_Z, shard, width), F32),
            pltpu.VMEM((shard, width), F32),
            pltpu.VMEM((shard, width), F32),
            dma((3,)), dma((total,)), dma((total,)), dma((total,)),
            dma((GROUP,)), dma((GROUP,)), dma((N_Z,)), dma((N_Z,)),
            dma((GROUP,)), dma((GROUP,)), dma((GROUP,)), dma((GROUP,)),
            dma((GROUP,)), dma((GROUP,)), dma((N_Z,)), dma((N_Z,)),
            dma, dma,
        ],
        compiler_params=pltpu.CompilerParams(
            collective_id=0, has_side_effects=True, vmem_limit_bytes=56 * 1024 * 1024),
        name="sections_and_loss",
    )(images, dw_kernel, dw_bias, norm_gain, norm_bias, w_in, b_in, w_out, b_out, layer_scale,
      image_embed, text_embed)
    return (section_out, row_lse.reshape(rows), col_lse.reshape(shard), grad_image, grad_text)


def solution(mesh):
    in_specs = (
        P("dp", None, None),
        P("pipe", None, None),
        P("pipe", None),
        P("pipe", None),
        P("pipe", None),
        P("pipe", None, None),
        P("pipe", None),
        P("pipe", None, None),
        P("pipe", None),
        P("pipe", None),
        P(("pipe", "dp"), None),
        P("dp", None),
    )
    out_specs = (
        P("pipe", "dp", None, None),
        P(("pipe", "dp")),
        P("dp"),
        P(("pipe", "dp"), None),
        P("dp", None),
    )
    return jax.shard_map(local, mesh=mesh, in_specs=in_specs, out_specs=out_specs, check_vma=False)
```

```python
import functools

import jax
import jax.numpy as jnp
from jax import lax
from jax.experimental import pallas as pl
from jax.experimental.pallas import tpu as pltpu
from jax.sharding import PartitionSpec as P

MESH = pl.DeviceIdType.MESH
F32 = jnp.float32
BF16 = jnp.bfloat16

N_Z, N_Y = 8, 4
GROUP = 16
SIDE = 32
LANES = 128
STRIP = 8
STRIPS = SIDE // STRIP
POS = STRIP * SIDE
LEFT = 8
CHUNK = 256


def kernel(
    images, dw_kernel, dw_bias, norm_gain, norm_bias, w_in, b_in, w_out, b_out, layer_scale,
    image_embed, text_embed,
    out, row_out, col_out, grad_image, grad_text,
    src, outbuf, xpad, taps, conv, normed, branch, w_in_v, w_out_v,
    imgbuf, txtbuf, imgf, img2, txt2, logit, logit_t, rowst, colst,
    gi_send, gi_recv, gt_send, gt_recv, gt_half, gt_other,
    load_sem, store_sem, strip_send, strip_recv, img_send, img_recv, txt_send, txt_recv,
    row_send, row_recv, col_send, col_recv, gis_sem, gir_sem, gts_sem, gtr_sem, half_send, half_recv,
):
    sec = lax.axis_index("pipe")
    dp = lax.axis_index("dp")
    core = lax.rem(dp, 2)
    y = lax.rem(lax.div(dp, 2), N_Y)
    z = lax.rem(lax.div(dp, 2 * N_Y), N_Z)
    x_lo = lax.div(dp, 2 * N_Y * N_Z)
    me_row = x_lo * 8 + y * 2 + core
    me_col = sec * N_Z + z
    micro = src.shape[0]
    channels = src.shape[2]
    tiles = channels // LANES
    hidden = w_in_v.shape[1]
    total = micro * STRIPS

    def row_peer(j):
        return (sec, ((lax.div(j, 8) * N_Z + z) * N_Y + lax.rem(lax.div(j, 2), N_Y)) * 2 + lax.rem(j, 2))

    def col_peer(j):
        return (lax.div(j, N_Z), ((x_lo * N_Z + lax.rem(j, N_Z)) * N_Y + y) * 2 + core)

    def text_peer(j):
        return (sec, ((x_lo * N_Z + j) * N_Y + y) * 2 + core)

    partner = (1 - sec, dp)

    def remote(source, target, send, recv, device):
        return pltpu.make_async_remote_copy(
            src_ref=source, dst_ref=target, send_sem=send, recv_sem=recv,
            device_id=device, device_id_type=MESH,
        )

    def others(count, me, act):
        def one(j, carry):
            @pl.when(j != me)
            def _():
                act(j)
            return carry
        lax.fori_loop(0, count, one, 0)

    load_x = pltpu.make_async_copy(images, src, load_sem.at[0])
    load_a = pltpu.make_async_copy(w_in.at[0], w_in_v, load_sem.at[1])
    load_b = pltpu.make_async_copy(w_out.at[0], w_out_v, load_sem.at[2])

    @pl.when(sec == 0)
    def _():
        load_x.start()
    load_a.start()
    load_b.start()

    barrier = pltpu.get_barrier_semaphore()
    others(GROUP, me_row, lambda j: pl.semaphore_signal(
        barrier, inc=1, device_id=row_peer(j), device_id_type=MESH))
    others(GROUP, me_col, lambda j: pl.semaphore_signal(
        barrier, inc=1, device_id=col_peer(j), device_id_type=MESH))

    def unit(values):
        wide = values.astype(F32)
        return (wide * lax.rsqrt(jnp.sum(wide * wide, axis=1, keepdims=True) + 1e-06)).astype(BF16)

    imgbuf[me_row] = unit(image_embed[...])
    txtbuf[z] = unit(text_embed[...])

    xpad[:, :, 0:3] = jnp.zeros(xpad.shape[:2] + (3,) + xpad.shape[3:], F32)
    xpad[:, :, SIDE + 3:SIDE + 6] = jnp.zeros(xpad.shape[:2] + (3,) + xpad.shape[3:], F32)
    xpad[:, :, :, 0:LEFT] = jnp.zeros(xpad.shape[:3] + (LEFT, LANES), F32)
    xpad[:, :, :, LEFT + SIDE:] = jnp.zeros(xpad.shape[:3] + (8, LANES), F32)
    kv = dw_kernel[0].astype(F32)
    for c in range(tiles):
        for t in range(49):
            taps[c, t] = jnp.broadcast_to(kv[t:t + 1, c * LANES:(c + 1) * LANES], (8, LANES))

    pl.semaphore_wait(barrier, 2 * (GROUP - 1))

    def img_copy(slot, j):
        return remote(imgbuf.at[slot], imgbuf.at[slot], img_send.at[j], img_recv.at[slot], row_peer(j))

    def txt_copy(slot, j):
        return remote(txtbuf.at[slot], txtbuf.at[slot], txt_send.at[j], txt_recv.at[slot], text_peer(j))

    def row_copy(slot, j):
        return remote(rowst.at[slot], rowst.at[slot], row_send.at[j], row_recv.at[slot], row_peer(j))

    def col_copy(slot, j):
        return remote(colst.at[slot], colst.at[slot], col_send.at[j], col_recv.at[slot], col_peer(j))

    def gi_copy(slot, j):
        return remote(gi_send.at[j], gi_recv.at[slot], gis_sem.at[j], gir_sem.at[slot], row_peer(j))

    def gt_copy(slot, j):
        return remote(gt_send.at[j], gt_recv.at[slot], gts_sem.at[j], gtr_sem.at[slot], text_peer(j))

    half_copy = remote(gt_half, gt_other, half_send, half_recv, partner)

    others(GROUP, me_row, lambda j: img_copy(me_row, j).start())
    others(N_Z, z, lambda j: txt_copy(z, j).start())

    def finish(copy):
        copy.wait_send()
        copy.wait_recv()

    lane = lax.broadcasted_iota(jnp.int32, (1, LANES), 1)
    low = lane < 64

    def loss_logits():
        others(GROUP, me_row, lambda j: finish(img_copy(j, j)))
        others(N_Z, z, lambda j: finish(txt_copy(j, j)))
        for j in range(GROUP):
            imgf[4 * j:4 * j + 4] = imgbuf[j].astype(F32)
        img = imgf[...].astype(BF16)
        img2[0:64] = img
        img2[64:128] = img
        for j in range(N_Z):
            imgf[8 * j:8 * j + 8] = txtbuf[j].astype(F32)
        txt = imgf[...].astype(BF16)
        txt2[0:64] = txt
        txt2[64:128] = txt
        dims = (((1,), (1,)), ((), ()))
        a = 100.0 * lax.dot_general(img2[0:64], txt2[...], dims, preferred_element_type=F32)
        b = 100.0 * lax.dot_general(txt2[0:64], img2[...], dims, preferred_element_type=F32)
        logit[...] = a
        logit_t[...] = b

        def stats(values):
            top = jnp.max(values, axis=0, keepdims=True)
            return jnp.where(low, top, jnp.sum(jnp.exp(values - top), axis=0, keepdims=True))

        colst[me_col] = stats(a)
        rowst[me_row] = stats(b)
        others(GROUP, me_row, lambda j: row_copy(me_row, j).start())
        others(GROUP, me_col, lambda j: col_copy(me_col, j).start())

    def merged(ref):
        parts = [ref[j] for j in range(GROUP)]
        top = functools.reduce(jnp.maximum, parts)
        add = functools.reduce(
            jnp.add, [pltpu.roll(p, 64, 1) * jnp.exp(jnp.where(low, p - top, 0.0)) for p in parts])
        lse = top + jnp.log(jnp.where(low, add, 1.0))
        return jnp.where(low, lse, pltpu.roll(lse, 64, 1))

    def upright(row):
        here = lax.broadcasted_iota(jnp.int32, (64, LANES), 0) == lax.broadcasted_iota(jnp.int32, (64, LANES), 1)
        return jnp.sum(jnp.where(here, row, 0.0), axis=1, keepdims=True)

    def image_ids(r):
        j = r >> 2
        peer = (((j >> 3) * N_Z + z) * N_Y + ((j >> 1) & 3)) * 2 + (j & 1)
        return (sec * 128 + peer) * 4 + (r & 3)

    def text_ids(r):
        return (((x_lo * N_Z + (r >> 3)) * N_Y + y) * 2 + core) * 8 + (r & 7)

    def loss_grads():
        others(GROUP, me_row, lambda j: finish(row_copy(j, j)))
        others(GROUP, me_col, lambda j: finish(col_copy(j, j)))
        row_lse = merged(rowst)
        col_lse = merged(colst)
        row_out[...] = pltpu.roll(row_lse, LANES - 4 * me_row, 1)[:, 0:4]
        col_out[...] = pltpu.roll(col_lse, LANES - 8 * z, 1)[:, 0:8]
        up = lax.broadcasted_iota(jnp.int32, (64, LANES), 0)
        across = lax.broadcasted_iota(jnp.int32, (64, LANES), 1)
        inside = across < 64
        a = logit[...]
        pair = image_ids(up) == text_ids(across)
        d = jnp.exp(a - upright(row_lse)) + jnp.exp(a - col_lse) - jnp.where(pair, 2.0, 0.0)
        d = jnp.where(inside, d, 0.0).astype(BF16)
        b = logit_t[...]
        pair_t = text_ids(up) == image_ids(across)
        dt = jnp.exp(b - row_lse) + jnp.exp(b - upright(col_lse)) - jnp.where(pair_t, 2.0, 0.0)
        dt = jnp.where(inside, dt, 0.0).astype(BF16)
        gi = 100.0 * jnp.dot(d, txt2[...], preferred_element_type=F32)
        gt = 100.0 * jnp.dot(dt, img2[...], preferred_element_type=F32)
        for j in range(GROUP):
            gi_send[j] = gi[4 * j:4 * j + 4]
        for j in range(N_Z):
            gt_send[j] = gt[8 * j:8 * j + 8]
        gi_recv[me_row] = gi_send[me_row]
        gt_recv[z] = gt_send[z]
        others(GROUP, me_row, lambda j: gi_copy(me_row, j).start())
        others(N_Z, z, lambda j: gt_copy(z, j).start())

    def loss_sums():
        others(GROUP, me_row, lambda j: finish(gi_copy(j, j)))
        others(N_Z, z, lambda j: finish(gt_copy(j, j)))
        grad_image[...] = functools.reduce(jnp.add, [gi_recv[j] for j in range(GROUP)])
        gt_half[...] = functools.reduce(jnp.add, [gt_recv[j] for j in range(N_Z)])
        half_copy.start()

    def strip_copy(n):
        i, s = lax.div(n, STRIPS), lax.rem(n, STRIPS)
        rows = pl.ds(pl.multiple_of(s * POS, POS), POS)
        return remote(outbuf.at[i, rows], src.at[i, rows], strip_send.at[n], strip_recv.at[n], (1, dp))

    def store_copy(n):
        i, s = lax.div(n, STRIPS), lax.rem(n, STRIPS)
        rows = pl.ds(pl.multiple_of(s * POS, POS), POS)
        return pltpu.make_async_copy(outbuf.at[i, rows], out.at[0, i, rows], store_sem.at[n])

    def arrive(n):
        i, s = lax.div(n, STRIPS), lax.rem(n, STRIPS)

        @pl.when(sec == 1)
        def _():
            strip_copy(n).wait_recv()
        v = src[i, pl.ds(pl.multiple_of(s * POS, POS), POS)].astype(F32)
        for c in range(tiles):
            xpad[i, c, pl.ds(3 + STRIP * s, STRIP), LEFT:LEFT + SIDE] = (
                v[:, c * LANES:(c + 1) * LANES].reshape(STRIP, SIDE, LANES))

    def block(i, s):
        def convolve(c, carry):
            for w in range(0, SIDE, 16):
                acc = jnp.zeros((STRIP, 2, 8, LANES), F32)
                for dw in range(7):
                    start = LEFT - 3 + dw + w
                    xs = xpad[i, c, pl.ds(STRIP * s, STRIP + 6), start:start + 16]
                    xs = xs.reshape(STRIP + 6, 2, 8, LANES)
                    for dh in range(7):
                        acc = acc + xs[dh:dh + STRIP] * taps[c, dh * 7 + dw]
                conv[c, :, w:w + 16] = acc.reshape(STRIP, 16, LANES)
            return carry

        lax.fori_loop(0, tiles, convolve, 0)

        def part(ref, c):
            return ref[0:1, c * LANES:(c + 1) * LANES].astype(F32)

        for q in range(4):
            rows = slice(q * POS // 4, (q + 1) * POS // 4)
            v = [conv[c, q * STRIP // 4:(q + 1) * STRIP // 4].reshape(POS // 4, LANES) + part(dw_bias, c)
                 for c in range(tiles)]
            mean = jnp.sum(functools.reduce(jnp.add, v), axis=1, keepdims=True) * (1.0 / channels)
            v = [a - mean for a in v]
            var = jnp.sum(functools.reduce(jnp.add, [a * a for a in v]), axis=1, keepdims=True) * (1.0 / channels)
            scale = lax.rsqrt(var + 1e-06)
            for c in range(tiles):
                normed[rows, c * LANES:(c + 1) * LANES] = (
                    v[c] * scale * part(norm_gain, c) + part(norm_bias, c)).astype(BF16)

        for n in range(hidden // CHUNK):
            cols = slice(n * CHUNK, (n + 1) * CHUNK)
            h = jnp.dot(normed[...], w_in_v[:, cols], preferred_element_type=F32)
            h = h + b_in[0:1, cols].astype(F32)
            g = (0.5 * h * (1.0 + lax.erf(h * 0.7071067811865476))).astype(BF16)
            p = jnp.dot(g, w_out_v[cols], preferred_element_type=F32)
            if n == 0:
                branch[...] = p
            else:
                branch[...] += p

        for c in range(tiles):
            cols = slice(c * LANES, (c + 1) * LANES)
            x = xpad[i, c, pl.ds(3 + STRIP * s, STRIP), LEFT:LEFT + SIDE].reshape(POS, LANES)
            r = x + part(layer_scale, c) * (branch[:, cols] + part(b_out, c))
            outbuf[i, pl.ds(pl.multiple_of(s * POS, POS), POS), cols] = r.astype(BF16)

    @pl.when(sec == 0)
    def _():
        load_x.wait()
    load_a.wait()
    load_b.wait()

    def strip(k):
        i, s = lax.div(k, STRIPS), lax.rem(k, STRIPS)

        @pl.when(s == 0)
        def _():
            arrive(k)

        @pl.when(s < STRIPS - 1)
        def _():
            arrive(k + 1)
        block(i, s)

        @pl.when(sec == 0)
        def _():
            strip_copy(k).start()
        store_copy(k).start()

    def step(k, carry):
        @pl.when(k == 1 - sec)
        def _():
            loss_logits()

        @pl.when(k == total * (1 - sec))
        def _():
            loss_grads()
            loss_sums()

        @pl.when(k < total)
        def _():
            strip(k)
        return carry

    lax.fori_loop(0, total + 1, step, 0)

    half_copy.wait_send()
    half_copy.wait_recv()
    grad_text[...] = gt_half[...] + gt_other[...]

    def drain(n, carry):
        store_copy(n).wait()

        @pl.when(sec == 0)
        def _():
            strip_copy(n).wait_send()
        return carry

    lax.fori_loop(0, total, drain, 0)


def local(images, dw_kernel, dw_bias, norm_gain, norm_bias, w_in, b_in, w_out, b_out, layer_scale,
          image_embed, text_embed):
    micro, positions, channels = images.shape
    hidden = w_in.shape[2]
    width = image_embed.shape[1]
    rows, shard = image_embed.shape[0], text_embed.shape[0]
    tiles = channels // LANES
    total = micro * STRIPS
    vmem = pl.BlockSpec(memory_space=pltpu.VMEM)
    hbm = pl.BlockSpec(memory_space=pl.ANY)
    dma = pltpu.SemaphoreType.DMA
    section_out, row_lse, col_lse, grad_image, grad_text = pl.pallas_call(
        kernel,
        out_shape=(
            jax.ShapeDtypeStruct((1,) + images.shape, BF16),
            jax.ShapeDtypeStruct((1, rows), F32),
            jax.ShapeDtypeStruct((1, shard), F32),
            jax.ShapeDtypeStruct((rows, width), F32),
            jax.ShapeDtypeStruct((shard, width), F32),
        ),
        in_specs=[hbm, vmem, vmem, vmem, vmem, hbm, vmem, hbm, vmem, vmem, vmem, vmem],
        out_specs=(hbm, vmem, vmem, vmem, vmem),
        scratch_shapes=[
            pltpu.VMEM(images.shape, BF16),
            pltpu.VMEM(images.shape, BF16),
            pltpu.VMEM((micro, tiles, SIDE + 6, LEFT + SIDE + 8, LANES), F32),
            pltpu.VMEM((tiles, 49, 8, LANES), F32),
            pltpu.VMEM((tiles, STRIP, SIDE, LANES), F32),
            pltpu.VMEM((POS, channels), BF16),
            pltpu.VMEM((POS, channels), F32),
            pltpu.VMEM((channels, hidden), BF16),
            pltpu.VMEM((hidden, channels), BF16),
            pltpu.VMEM((GROUP, rows, width), BF16),
            pltpu.VMEM((N_Z, shard, width), BF16),
            pltpu.VMEM((64, width), F32),
            pltpu.VMEM((128, width), BF16),
            pltpu.VMEM((128, width), BF16),
            pltpu.VMEM((64, LANES), F32),
            pltpu.VMEM((64, LANES), F32),
            pltpu.VMEM((GROUP, 1, LANES), F32),
            pltpu.VMEM((GROUP, 1, LANES), F32),
            pltpu.VMEM((GROUP, rows, width), F32),
            pltpu.VMEM((GROUP, rows, width), F32),
            pltpu.VMEM((N_Z, shard, width), F32),
            pltpu.VMEM((N_Z, shard, width), F32),
            pltpu.VMEM((shard, width), F32),
            pltpu.VMEM((shard, width), F32),
            dma((3,)), dma((total,)), dma((total,)), dma((total,)),
            dma((GROUP,)), dma((GROUP,)), dma((N_Z,)), dma((N_Z,)),
            dma((GROUP,)), dma((GROUP,)), dma((GROUP,)), dma((GROUP,)),
            dma((GROUP,)), dma((GROUP,)), dma((N_Z,)), dma((N_Z,)),
            dma, dma,
        ],
        compiler_params=pltpu.CompilerParams(
            collective_id=0, has_side_effects=True, vmem_limit_bytes=56 * 1024 * 1024),
        name="sections_and_loss",
    )(images, dw_kernel, dw_bias, norm_gain, norm_bias, w_in, b_in, w_out, b_out, layer_scale,
      image_embed, text_embed)
    return (section_out, row_lse.reshape(rows), col_lse.reshape(shard), grad_image, grad_text)


def solution(mesh):
    in_specs = (
        P("dp", None, None),
        P("pipe", None, None),
        P("pipe", None),
        P("pipe", None),
        P("pipe", None),
        P("pipe", None, None),
        P("pipe", None),
        P("pipe", None, None),
        P("pipe", None),
        P("pipe", None),
        P(("pipe", "dp"), None),
        P("dp", None),
    )
    out_specs = (
        P("pipe", "dp", None, None),
        P(("pipe", "dp")),
        P("dp"),
        P(("pipe", "dp"), None),
        P("dp", None),
    )
    return jax.shard_map(local, mesh=mesh, in_specs=in_specs, out_specs=out_specs, check_vma=False)
```
